32 devices in a mesh: segment: 4 (over x, core), strip: 8 (over z, y).
Axes of the slice: x: 2, y: 2, z: 4, core: 2. Of those that a mesh axis runs over, the one named last changes fastest.
Arguments:
- held_blocks: bfloat16 [4, 4, 64, 12, 384], P('segment', None, 'strip'), may hold values from -6 to 6
- incoming: bfloat16 [1, 4, 64, 12, 384], P(None, None, 'strip'), may hold values from -6 to 6
- frame_counts: int32 [5], replicated, may hold values from 1 to 4, as said below
- first_cache: bfloat16 [4, 2, 64, 12, 384], P('segment', None, 'strip'), may hold values from -0.25 to 2
- second_cache: bfloat16 [4, 2, 64, 12, 384], P('segment', None, 'strip'), may hold values from -0.25 to 2
- first_kernel: bfloat16 [4, 3, 3, 3, 384, 384], P('segment'), may hold values from -0.0625 to 0.0625
- first_bias: float32 [4, 384], P('segment'), may hold values from -3 to 3
- first_gain: float32 [4, 384], P('segment'), may hold values from 0.5 to 2
- second_kernel: bfloat16 [4, 3, 3, 3, 384, 384], P('segment'), may hold values from -0.0625 to 0.0625
- second_bias: float32 [4, 384], P('segment'), may hold values from -3 to 3
- second_gain: float32 [4, 384], P('segment'), may hold values from 0.5 to 2
Outputs:
- section_out: bfloat16 [2, 4, 4, 64, 12, 384], P(None, 'segment', None, 'strip')
- first_cache_out: bfloat16 [4, 2, 64, 12, 384], P('segment', None, 'strip')
- second_cache_out: bfloat16 [4, 2, 64, 12, 384], P('segment', None, 'strip')
The draws below stay inside these ranges and needn't reach their ends.
Inputs may be any that keep to these rules, and one draw needn't show every extreme that they name: `frame_counts`: the section at segment index s works at tick t (from 0) on block 3 - s + t; both 1 and 4 occur in every draw.
All inputs are finite; a program needn't handle non-finite values.
Results may differ from the reference program's by a relative error of at most 0.0051.
Values may be sent and summed in bfloat16 or wider, within the bound.
A program may use at most 128 MiB of HBM per device.

```python
import math
import jax
import jax.numpy as jnp
from jax import lax

C = 384
FMAX = 4
TICKS = 2
COLS = 12
HEIGHT = 64
SECTIONS = 4
BLOCKS = 5


def draw_frame_counts(key, part):
    counts = jax.random.randint(jax.random.fold_in(key, 11), (BLOCKS,), 1, FMAX + 1)
    top_place = jax.random.randint(jax.random.fold_in(key, 12), (), 0, BLOCKS)
    low_offset = jax.random.randint(jax.random.fold_in(key, 13), (), 1, BLOCKS)
    low_place = (top_place + low_offset) % BLOCKS
    positions = jnp.arange(BLOCKS)
    counts = jnp.where(positions == top_place, FMAX, counts)
    counts = jnp.where(positions == low_place, 1, counts)
    return counts.astype(jnp.int32)


def shard_levels(rng, shape, pieces, least, top_value):
    loudness, own = 1.0, jax.random.fold_in(rng, 6)
    for axis_at, blocks in pieces:
        steps = jnp.exp(jax.random.uniform(jax.random.fold_in(own, axis_at), (blocks,), jnp.float32, least / len(pieces), top_value / len(pieces)))
        loudness = loudness * jnp.repeat(steps, shape[axis_at] // blocks).reshape([-1 if axis == axis_at else 1 for axis in range(len(shape))])
    return loudness


def gaussian(key, dims, deviation, most, cuts=(), held_as=jnp.bfloat16):
    array = deviation * jax.random.normal(key, dims, jnp.float32)
    if cuts:
        array = array * shard_levels(key, dims, cuts, -0.22, 0.18)
    return jnp.clip(array, -most, most).astype(held_as)


def setup_inputs(seed: int = 0) -> dict:
    splits = jax.random.split(jax.random.key(seed), 12)
    return {
        "held_blocks": gaussian(splits[0], (SECTIONS, FMAX, HEIGHT, COLS, C), 1.0, 6.0, ((0, 4), (2, 8))),
        "incoming": gaussian(splits[1], (TICKS - 1, FMAX, HEIGHT, COLS, C), 1.0, 6.0, ((2, 8),)),
        "frame_counts": draw_frame_counts(jax.random.fold_in(splits[11], 71), 0),
        "first_cache": jnp.clip(-0.25 + 2.25 * jax.random.uniform(splits[3], (SECTIONS, 2, HEIGHT, COLS, C), jnp.float32) ** shard_levels(splits[3], (SECTIONS, 2, HEIGHT, COLS, C), ((0, 4), (2, 8)), -0.2, 0.2), -0.25, 2.0).astype(jnp.bfloat16),
        "second_cache": jnp.clip(-0.25 + 2.25 * jax.random.uniform(splits[4], (SECTIONS, 2, HEIGHT, COLS, C), jnp.float32) ** shard_levels(splits[4], (SECTIONS, 2, HEIGHT, COLS, C), ((0, 4), (2, 8)), -0.2, 0.2), -0.25, 2.0).astype(jnp.bfloat16),
        "first_kernel": gaussian(splits[5], (SECTIONS, 3, 3, 3, C, C), (27 * C) ** -0.5, 0.0625, ((0, 4),)),
        "first_bias": gaussian(splits[6], (SECTIONS, C), 0.5, 3.0, ((0, 4),), jnp.float32),
        "first_gain": jnp.clip(jnp.exp(math.log(2.0) - 1.3862944 * jax.random.uniform(splits[7], (SECTIONS, C), jnp.float32) ** shard_levels(splits[7], (SECTIONS, C), ((0, 4),), -0.2, 0.2)), 0.5, 2.0),
        "second_kernel": gaussian(splits[8], (SECTIONS, 3, 3, 3, C, C), (27 * C) ** -0.5, 0.0625, ((0, 4),)),
        "second_bias": gaussian(splits[9], (SECTIONS, C), 0.5, 3.0, ((0, 4),), jnp.float32),
        "second_gain": jnp.clip(jnp.exp(math.log(2.0) - 1.3862944 * jax.random.uniform(splits[10], (SECTIONS, C), jnp.float32) ** shard_levels(splits[10], (SECTIONS, C), ((0, 4),), -0.2, 0.2)), 0.5, 2.0),
    }


EPSILON = 1e-06

def normed(values, channel_gain):
    factor = lax.rsqrt(lax.optimization_barrier(jnp.mean(values * values, axis=-1, keepdims=True)) + EPSILON)
    return jax.nn.silu(values * factor * channel_gain)

def convolve(window, kernel, frames):
    out_rows = window.shape[1] - 2
    breadth = window.shape[2]
    channels = kernel.shape[-1]
    padded = jnp.pad(window, ((0, 0), (0, 0), (1, 1), (0, 0)))
    summed = jnp.zeros((frames * out_rows * breadth, channels), jnp.float32)
    for time_tap in range(3):
        for row_tap in range(3):
            stacked = jnp.concatenate([padded[time_tap:time_tap + frames, row_tap:row_tap + out_rows, col_tap:col_tap + breadth] for col_tap in range(3)], axis=-1)
            summed = summed + jnp.dot(stacked.reshape(-1, 3 * channels), kernel[time_tap, row_tap].reshape(3 * channels, channels), preferred_element_type=jnp.float32)
    return summed.reshape(frames, out_rows, breadth, channels)

def section(current, live_count, first_cache, second_cache, first_kernel, first_bias, first_gain, second_kernel, second_bias, second_gain):
    frames = current.shape[0]
    live_mask = (jnp.arange(frames) < live_count)[:, None, None, None]
    inputs = jnp.where(live_mask, current.astype(jnp.float32), 0.0)
    first_in = normed(inputs, first_gain).astype(jnp.bfloat16)
    first_window = jnp.concatenate([first_cache, first_in], axis=0)
    first_rimmed = jnp.pad(first_window, ((0, 0), (1, 1), (0, 0), (0, 0)))
    hidden = jnp.where(live_mask, convolve(first_rimmed, first_kernel, frames) + first_bias, 0.0)
    second_in = normed(hidden, second_gain).astype(jnp.bfloat16)
    second_window = jnp.concatenate([second_cache, second_in], axis=0)
    second_rimmed = jnp.pad(second_window, ((0, 0), (1, 1), (0, 0), (0, 0)))
    result = jnp.where(live_mask, inputs + convolve(second_rimmed, second_kernel, frames) + second_bias, 0.0).astype(jnp.bfloat16)
    first_next = lax.dynamic_slice_in_dim(first_window, live_count, 2, 0)
    second_next = lax.dynamic_slice_in_dim(second_window, live_count, 2, 0)
    return (result, first_next, second_next)

def reference(held_blocks, incoming, frame_counts, first_cache, second_cache, first_kernel, first_bias, first_gain, second_kernel, second_bias, second_gain):
    sections = held_blocks.shape[0]
    current = held_blocks
    first_state = first_cache
    second_state = second_cache
    produced = []
    for tick_index in range(TICKS):
        if tick_index > 0:
            current = jnp.concatenate([incoming[tick_index - 1][None], produced[-1][:-1]], axis=0)
        counts_now = frame_counts[tick_index:tick_index + sections][::-1].astype(jnp.int32)

        def advance(carried, members):
            outcome = section(members[0], members[1], members[2], members[3], members[4], members[5], members[6], members[7], members[8], members[9])
            return (carried, outcome)
        unused, stacked_out = lax.scan(advance, jnp.zeros((), jnp.int32), (current, counts_now, first_state, second_state, first_kernel, first_bias, first_gain, second_kernel, second_bias, second_gain))
        outputs, first_state, second_state = stacked_out
        produced.append(outputs)
    return (jnp.stack(produced), first_state, second_state)
```

```python
import jax
import jax.numpy as jnp
from jax import lax
from jax.experimental import pallas as pl
from jax.experimental.pallas import tpu as pltpu
from jax.sharding import PartitionSpec as P

EPSILON = 1e-06
MESH = pl.DeviceIdType.MESH


def normed(values, channel_gain):
    factor = lax.rsqrt(jnp.mean(values * values, axis=-1, keepdims=True) + EPSILON)
    half = values * factor * (0.5 * channel_gain)
    return half + half * jnp.tanh(half)


def with_neighbours(values, above, below):
    height = values.shape[1]
    row = lax.broadcasted_iota(jnp.int32, values.shape[:2] + (1,), 1)
    down = jnp.where(row == 0, above, pltpu.roll(values, 1, 1))
    up = jnp.where(row == height - 1, below, pltpu.roll(values, height - 1, 1))
    return down, up


def kernel(
    counts, held, incoming, first_cache, second_cache, first_kernel, first_bias, first_gain,
    second_kernel, second_bias, second_gain, out, first_out, second_out,
    raw, raw_edge, fcache, fcache_edge, scache, scache_edge, second_in, second_edge,
    x1, x2, w1, w2, acc, local_sem, w_sem, send_sem, recv_sem,
):
    ticks, frames, cols, height, channels = (out.shape[i] for i in (0, 2, 3, 4, 5))
    half = frames // 2
    sections, strips = lax.axis_size("segment"), lax.axis_size("strip")
    s, p = lax.axis_index("segment"), lax.axis_index("strip")
    has_above, has_below = p > 0, p < strips - 1
    f32, bf16 = jnp.float32, jnp.bfloat16

    local = [
        pltpu.make_async_copy(held.at[0], raw.at[0], local_sem.at[0]),
        pltpu.make_async_copy(first_cache.at[0], fcache, local_sem.at[1]),
        pltpu.make_async_copy(second_cache.at[0], scache, local_sem.at[2]),
    ]
    for copy in local:
        copy.start()
    fresh = pltpu.make_async_copy(incoming.at[0], raw.at[1], local_sem.at[3])

    def weight(source, target, which, a, b, c):
        return pltpu.make_async_copy(
            source.at[0, a, b, c],
            target.at[pl.ds((a * 3 + b) * channels, channels), pl.ds(c * channels, channels)],
            w_sem.at[which],
        )

    taps = [(a, b, c) for a in range(3) for b in range(3) for c in range(3)]
    around = [(i, j) for i in (-1, 0, 1) for j in (-1, 0, 1) if (i, j) != (0, 0)]
    barrier = pltpu.get_barrier_semaphore()

    def exists(i, j):
        return (s + i >= 0) & (s + i < sections) & (p + j >= 0) & (p + j < strips)

    for i, j in around:
        @pl.when(exists(i, j))
        def _(i=i, j=j):
            pl.semaphore_signal(barrier, inc=1, device_id=(s + i, p + j), device_id_type=MESH)

    for tap in taps:
        weight(first_kernel, w1, 0, *tap).start()

    pl.semaphore_wait(barrier, sum(exists(i, j).astype(jnp.int32) for i, j in around))

    def remote(source, target, k, i, j):
        return pltpu.make_async_remote_copy(
            src_ref=source, dst_ref=target, send_sem=send_sem.at[k], recv_sem=recv_sem.at[k],
            device_id=(s + i, p + j), device_id_type=MESH,
        )

    low, high = pl.ds(0, 2), pl.ds(height - 2, 2)

    def edge(source, target, side, k, i):
        rows, j = (high, 1) if side == 0 else (low, -1)
        return remote(source.at[:, :, rows], target, k + side, i, j)

    def start_edges(side):
        return [
            edge(first_cache.at[0], fcache_edge.at[side], side, 2, 0),
            edge(held.at[0], raw_edge.at[0, side], side, 0, 0),
            edge(second_cache.at[0], scache_edge.at[side], side, 4, 0),
        ]

    def fresh_edge(side):
        return edge(incoming.at[0], raw_edge.at[1, side], side, 6, 0)

    def span(h):
        return pl.ds(h * half, half)

    def block(h):
        return remote(out.at[0, 0, span(h)], raw.at[1, span(h)], 8 + h, 1, 0)

    def block_edge(h, side):
        target = raw_edge.at[1, side, span(h)]
        return edge(out.at[0, 0, span(h)], target, side, 10 + 2 * h, 1)

    def second_rows(tick, h, side):
        target = second_edge.at[tick, side, span(h)]
        return edge(second_in.at[tick, span(h)], target, side, 14 + 4 * tick + 2 * h, 0)

    sends_to = (has_below, has_above)
    takes_from = (has_above, has_below)
    for side in range(2):
        @pl.when(sends_to[side])
        def _(side=side):
            for copy in start_edges(side):
                copy.start()

    @pl.when(s == 0)
    def _():
        fresh.start()
        for side in range(2):
            @pl.when(sends_to[side])
            def _(side=side):
                fresh_edge(side).start()

    for tap in taps:
        weight(second_kernel, w2, 1, *tap).start()

    acc[:, 0] = jnp.zeros((half, height, 3 * channels), f32)
    acc[:, cols + 1] = jnp.zeros((half, height, 3 * channels), f32)
    for side in range(2):
        @pl.when(jnp.logical_not(takes_from[side]))
        def _(side=side):
            raw_edge[:, side] = jnp.zeros((ticks, frames, cols, 2, channels), bf16)
            second_edge[:, side] = jnp.zeros((ticks, frames, cols, 2, channels), bf16)
            fcache_edge[side] = jnp.zeros((2, cols, 2, channels), bf16)
            scache_edge[side] = jnp.zeros((2, cols, 2, channels), bf16)

    def put(window, f, b, values):
        flat = values.reshape(cols * height, channels).astype(bf16)
        window[f, :, b * channels : (b + 1) * channels] = flat

    def edges_of(ref_above, ref_below):
        shape = (cols, 2, channels)
        which = lax.broadcasted_iota(jnp.int32, shape, 1)
        return jnp.where(which == 1, ref_above.astype(f32), ref_below.astype(f32))

    for copy in local:
        copy.wait()
    for side in range(2):
        @pl.when(takes_from[side])
        def _(side=side):
            for copy in start_edges(side):
                copy.wait_recv()

    for window, cache, rows in ((x1, fcache, fcache_edge), (x2, scache, scache_edge)):
        for f in range(2):
            values = cache[f].astype(f32)
            pair = edges_of(rows[0, f], rows[1, f])
            down, up = with_neighbours(values, pair[:, 1:2], pair[:, 0:1])
            for b, shifted in enumerate((down, values, up)):
                put(window, f, b, shifted)

    def convolve(window, weights, h):
        lhs = jnp.concatenate(
            [
                window[pl.ds(h * half + a, half)].reshape(half * cols * height, 3 * channels)
                for a in range(3)
            ],
            axis=-1,
        )
        product = jnp.dot(lhs, weights[...], preferred_element_type=f32)
        acc[:, 1 : cols + 1] = product.reshape(half, cols, height, 3 * channels)

    def summed(f, bias):
        return (
            acc[f, 0:cols, :, 0:channels]
            + acc[f, 1 : cols + 1, :, channels : 2 * channels]
            + acc[f, 2 : cols + 2, :, 2 * channels : 3 * channels]
            + bias
        )

    @pl.loop(0, ticks)
    def _(tick):
        live = counts[sections - 1 - s + tick]

        @pl.loop(0, 2)
        def _(h):
            @pl.when((tick > 0) & (s == 0) & (h == 0))
            def _():
                fresh.wait()
                for side in range(2):
                    @pl.when(takes_from[side])
                    def _(side=side):
                        fresh_edge(side).wait_recv()

            @pl.when((tick > 0) & (s > 0))
            def _():
                block(h).wait_recv()
                for side in range(2):
                    @pl.when(takes_from[side])
                    def _(side=side):
                        block_edge(h, side).wait_recv()

            @pl.loop(0, half)
            def _(i):
                f = h * half + i
                alive = f < live
                values = normed(jnp.where(alive, raw[tick, f].astype(f32), 0.0), first_gain[...])
                pair = edges_of(raw_edge[tick, 0, f], raw_edge[tick, 1, f])
                pair = normed(jnp.where(alive, pair, 0.0), first_gain[...])
                down, up = with_neighbours(values, pair[:, 1:2], pair[:, 0:1])
                for b, shifted in enumerate((down, values, up)):
                    put(x1, 2 + f, b, shifted)

            @pl.when((tick == 0) & (h == 0))
            def _():
                for tap in taps:
                    weight(first_kernel, w1, 0, *tap).wait()

            convolve(x1, w1, h)

            @pl.loop(0, half)
            def _(i):
                f = h * half + i
                hidden = jnp.where(f < live, summed(i, first_bias[...]), 0.0)
                values = normed(hidden, second_gain[...])
                second_in[tick, f] = values.astype(bf16)
                put(x2, 2 + f, 1, values)

            for side in range(2):
                @pl.when(sends_to[side])
                def _(side=side):
                    second_rows(tick, h, side).start()

        @pl.loop(0, 2)
        def _(h):
            for side in range(2):
                @pl.when(takes_from[side])
                def _(side=side):
                    second_rows(tick, h, side).wait_recv()

            @pl.loop(0, half)
            def _(i):
                f = h * half + i
                values = second_in[tick, f].astype(f32)
                pair = edges_of(second_edge[tick, 0, f], second_edge[tick, 1, f])
                down, up = with_neighbours(values, pair[:, 1:2], pair[:, 0:1])
                put(x2, 2 + f, 0, down)
                put(x2, 2 + f, 2, up)

            @pl.when((tick == 0) & (h == 0))
            def _():
                for tap in taps:
                    weight(second_kernel, w2, 1, *tap).wait()

            convolve(x2, w2, h)

            @pl.loop(0, half)
            def _(i):
                f = h * half + i
                total = summed(i, second_bias[...]) + raw[tick, f].astype(f32)
                out[tick, 0, f] = jnp.where(f < live, total, 0.0).astype(bf16)

            @pl.when((tick == 0) & (s < sections - 1))
            def _():
                block(h).start()
                for side in range(2):
                    @pl.when(sends_to[side])
                    def _(side=side):
                        block_edge(h, side).start()

        for window in (x1, x2):
            for j in range(2):
                window[j] = window[live + j]

    for window, target in ((x1, first_out), (x2, second_out)):
        for j in range(2):
            values = window[j, :, channels : 2 * channels].astype(f32)
            target[0, j] = values.reshape(cols, height, channels).astype(bf16)

    for side in range(2):
        @pl.when(sends_to[side])
        def _(side=side):
            for copy in start_edges(side):
                copy.wait_send()

            @pl.loop(0, ticks)
            def _(tick):
                for h in range(2):
                    second_rows(tick, h, side).wait_send()

            @pl.when(s == 0)
            def _():
                fresh_edge(side).wait_send()

            @pl.when(s < sections - 1)
            def _():
                for h in range(2):
                    block_edge(h, side).wait_send()

    @pl.when(s < sections - 1)
    def _():
        for h in range(2):
            block(h).wait_send()


def deliver(*refs):
    sem = refs[-1]
    copies = [
        pltpu.make_async_copy(refs[k], refs[3 + k], sem.at[k]) for k in range(3)
    ]
    for copy in copies:
        copy.start()
    for copy in copies:
        copy.wait()


def swapped(array):
    return jnp.swapaxes(array, -3, -2)


def on_device(
    held_blocks, incoming, frame_counts, first_cache, second_cache, first_kernel, first_bias,
    first_gain, second_kernel, second_bias, second_gain,
):
    held_blocks, incoming, first_cache, second_cache = (
        swapped(v) for v in (held_blocks, incoming, first_cache, second_cache)
    )
    _, frames, cols, height, channels = held_blocks.shape
    ticks = incoming.shape[0] + 1
    bf16 = jnp.bfloat16
    anywhere = pl.BlockSpec(memory_space=pltpu.HBM)
    inside = pl.BlockSpec(memory_space=pltpu.VMEM)
    shapes = (
        jax.ShapeDtypeStruct((ticks, 1, frames, cols, height, channels), bf16),
        jax.ShapeDtypeStruct(first_cache.shape, bf16),
        jax.ShapeDtypeStruct(second_cache.shape, bf16),
    )
    transfers = 14 + 4 * ticks
    results = pl.pallas_call(
        kernel,
        out_shape=shapes,
        in_specs=[pl.BlockSpec(memory_space=pltpu.SMEM)] + [anywhere] * 5
        + [inside, inside, anywhere, inside, inside],
        out_specs=(inside, inside, inside),
        scratch_shapes=[
            pltpu.VMEM((ticks, frames, cols, height, channels), bf16),
            pltpu.VMEM((ticks, 2, frames, cols, 2, channels), bf16),
            pltpu.VMEM((2, cols, height, channels), bf16),
            pltpu.VMEM((2, 2, cols, 2, channels), bf16),
            pltpu.VMEM((2, cols, height, channels), bf16),
            pltpu.VMEM((2, 2, cols, 2, channels), bf16),
            pltpu.VMEM((ticks, frames, cols, height, channels), bf16),
            pltpu.VMEM((ticks, 2, frames, cols, 2, channels), bf16),
            pltpu.VMEM((frames + 2, cols * height, 3 * channels), bf16),
            pltpu.VMEM((frames + 2, cols * height, 3 * channels), bf16),
            pltpu.VMEM((9 * channels, 3 * channels), bf16),
            pltpu.VMEM((9 * channels, 3 * channels), bf16),
            pltpu.VMEM((frames // 2, cols + 2, height, 3 * channels), jnp.float32),
            pltpu.SemaphoreType.DMA((4,)),
            pltpu.SemaphoreType.DMA((2,)),
            pltpu.SemaphoreType.DMA((transfers,)),
            pltpu.SemaphoreType.DMA((transfers,)),
        ],
        compiler_params=pltpu.CompilerParams(
            collective_id=0, has_side_effects=True, vmem_limit_bytes=60 * 1024 * 1024
        ),
    )(
        frame_counts, held_blocks, incoming, first_cache, second_cache, first_kernel, first_bias,
        first_gain, second_kernel, second_bias, second_gain,
    )
    results = pl.pallas_call(
        deliver,
        out_shape=shapes,
        in_specs=[inside] * 3,
        out_specs=(anywhere,) * 3,
        scratch_shapes=[pltpu.SemaphoreType.DMA((3,))],
        compiler_params=pltpu.CompilerParams(vmem_limit_bytes=4 * 1024 * 1024),
    )(*results)
    return tuple(swapped(v) for v in results)


def solution(mesh):
    return jax.shard_map(
        on_device,
        mesh=mesh,
        in_specs=(
            P("segment", None, "strip", None, None),
            P(None, None, "strip", None, None),
            P(),
            P("segment", None, "strip", None, None),
            P("segment", None, "strip", None, None),
            P("segment", None, None, None, None, None),
            P("segment", None),
            P("segment", None),
            P("segment", None, None, None, None, None),
            P("segment", None),
            P("segment", None),
        ),
        out_specs=(
            P(None, "segment", None, "strip", None, None),
            P("segment", None, "strip", None, None),
            P("segment", None, "strip", None, None),
        ),
        check_vma=False,
    )
```

```python
import jax
import jax.numpy as jnp
from jax import lax
from jax.experimental import pallas as pl
from jax.experimental.pallas import tpu as pltpu
from jax.sharding import PartitionSpec as P

EPSILON = 1e-06
MESH = pl.DeviceIdType.MESH


def normed(values, channel_gain):
    factor = lax.rsqrt(jnp.mean(values * values, axis=-1, keepdims=True) + EPSILON)
    half = values * factor * (0.5 * channel_gain)
    return half + half * jnp.tanh(half)


def with_neighbours(values, above, below):
    height = values.shape[1]
    row = lax.broadcasted_iota(jnp.int32, values.shape[:2] + (1,), 1)
    down = jnp.where(row == 0, above, pltpu.roll(values, 1, 1))
    up = jnp.where(row == height - 1, below, pltpu.roll(values, height - 1, 1))
    return down, up


def kernel(
    counts, held, incoming, first_cache, second_cache, first_kernel, first_bias, first_gain,
    second_kernel, second_bias, second_gain, out, first_out, second_out,
    raw, raw_edge, fcache, fcache_edge, scache, scache_edge, second_in, second_edge,
    x1, x2, w1, w2, acc, local_sem, w_sem, send_sem, recv_sem,
):
    ticks, frames, cols, height, channels = (out.shape[i] for i in (0, 2, 3, 4, 5))
    half = frames // 2
    sections, strips = lax.axis_size("segment"), lax.axis_size("strip")
    s, p = lax.axis_index("segment"), lax.axis_index("strip")
    has_above, has_below = p > 0, p < strips - 1
    f32, bf16 = jnp.float32, jnp.bfloat16

    local = [
        pltpu.make_async_copy(held.at[0], raw.at[0], local_sem.at[0]),
        pltpu.make_async_copy(first_cache.at[0], fcache, local_sem.at[1]),
        pltpu.make_async_copy(second_cache.at[0], scache, local_sem.at[2]),
    ]
    for copy in local:
        copy.start()
    fresh = pltpu.make_async_copy(incoming.at[0], raw.at[1], local_sem.at[3])

    def weights(source, target, which, blocks, start):
        return [
            pltpu.make_async_copy(
                source.at[0, a, b, c],
                target.at[pl.ds((start + k) * channels, channels), pl.ds(c * channels, channels)],
                w_sem.at[which],
            )
            for k, (a, b) in enumerate(blocks)
            for c in range(3)
        ]

    first_a = [(0, 1), (1, 1), (2, 1)]
    first_b = [(a, b) for a in range(3) for b in (0, 2)]
    second_a = [(0, 1), (0, 0), (0, 2), (1, 1), (2, 1)]
    second_b = [(a, b) for a in (1, 2) for b in (0, 2)]
    loads = [
        weights(first_kernel, w1, 0, first_a, 0),
        weights(first_kernel, w1, 1, first_b, len(first_a)),
        weights(second_kernel, w2, 2, second_a, 0),
        weights(second_kernel, w2, 3, second_b, len(second_a)),
    ]
    around = [(i, j) for i in (-1, 0, 1) for j in (-1, 0, 1) if (i, j) != (0, 0)]
    barrier = pltpu.get_barrier_semaphore()

    def exists(i, j):
        return (s + i >= 0) & (s + i < sections) & (p + j >= 0) & (p + j < strips)

    for i, j in around:
        @pl.when(exists(i, j))
        def _(i=i, j=j):
            pl.semaphore_signal(barrier, inc=1, device_id=(s + i, p + j), device_id_type=MESH)

    for copy in loads[0]:
        copy.start()

    pl.semaphore_wait(barrier, sum(exists(i, j).astype(jnp.int32) for i, j in around))

    def remote(source, target, k, i, j):
        return pltpu.make_async_remote_copy(
            src_ref=source, dst_ref=target, send_sem=send_sem.at[k], recv_sem=recv_sem.at[k],
            device_id=(s + i, p + j), device_id_type=MESH,
        )

    low, high = pl.ds(0, 2), pl.ds(height - 2, 2)

    def edge(source, target, side, k, i):
        rows, j = (high, 1) if side == 0 else (low, -1)
        return remote(source.at[:, :, rows], target, k + side, i, j)

    def start_edges(side):
        return [
            edge(first_cache.at[0], fcache_edge.at[side], side, 2, 0),
            edge(held.at[0], raw_edge.at[0, side], side, 0, 0),
            edge(second_cache.at[0], scache_edge.at[side], side, 4, 0),
        ]

    def fresh_edge(side):
        return edge(incoming.at[0], raw_edge.at[1, side], side, 6, 0)

    def span(h):
        return pl.ds(h * half, half)

    def block(h):
        return remote(out.at[0, 0, span(h)], raw.at[1, span(h)], 8 + h, 1, 0)

    def block_edge(h, side):
        target = raw_edge.at[1, side, span(h)]
        return edge(out.at[0, 0, span(h)], target, side, 10 + 2 * h, 1)

    def second_rows(tick, h, side):
        target = second_edge.at[tick, side, span(h)]
        return edge(second_in.at[tick, span(h)], target, side, 14 + 4 * tick + 2 * h, 0)

    sends_to = (has_below, has_above)
    takes_from = (has_above, has_below)
    for side in range(2):
        @pl.when(sends_to[side])
        def _(side=side):
            for copy in start_edges(side):
                copy.start()

    @pl.when(s == 0)
    def _():
        fresh.start()
        for side in range(2):
            @pl.when(sends_to[side])
            def _(side=side):
                fresh_edge(side).start()

    for copy in loads[1]:
        copy.start()

    for h in range(2):
        for at in (0, cols + 1):
            acc[h, :, at] = jnp.zeros((half, height, 3 * channels), f32)
    for side in range(2):
        @pl.when(jnp.logical_not(takes_from[side]))
        def _(side=side):
            raw_edge[:, side] = jnp.zeros((ticks, frames, cols, 2, channels), bf16)
            second_edge[:, side] = jnp.zeros((ticks, frames, cols, 2, channels), bf16)
            fcache_edge[side] = jnp.zeros((2, cols, 2, channels), bf16)
            scache_edge[side] = jnp.zeros((2, cols, 2, channels), bf16)

    def put(window, f, plane, values):
        flat = values.reshape(cols * height, channels).astype(bf16)
        window[f, :, plane * channels : (plane + 1) * channels] = flat

    def put_shifted(window, f, above, below, prepare):
        values = window[f, :, 0:channels].astype(f32).reshape(cols, height, channels)
        which = lax.broadcasted_iota(jnp.int32, (cols, 2, channels), 1)
        pair = prepare(jnp.where(which == 1, above.astype(f32), below.astype(f32)))
        down, up = with_neighbours(values, pair[:, 1:2], pair[:, 0:1])
        put(window, f, 1, down)
        put(window, f, 2, up)

    for copy in local:
        copy.wait()
    for window, cache in ((x1, fcache), (x2, scache)):
        for f in range(2):
            put(window, f, 0, cache[f].astype(f32))

    def part(window, matrix, h, pieces, start):
        lhs = jnp.concatenate(
            [
                window[pl.ds(h * half + a, half), :, first * channels : last * channels].reshape(
                    half * cols * height, (last - first) * channels
                )
                for a, first, last in pieces
            ],
            axis=-1,
        )
        rows = matrix[start * channels : start * channels + lhs.shape[-1]]
        product = jnp.dot(lhs, rows, preferred_element_type=f32)
        return product.reshape(half, cols, height, 3 * channels)

    def summed(h, f, bias):
        return (
            acc[h, f, 0:cols, :, 0:channels]
            + acc[h, f, 1 : cols + 1, :, channels : 2 * channels]
            + acc[h, f, 2 : cols + 2, :, 2 * channels : 3 * channels]
            + bias
        )

    @pl.loop(0, ticks)
    def _(tick):
        live = counts[sections - 1 - s + tick]

        def first_start(h):
            @pl.when((tick > 0) & (s == 0) & (h == 0))
            def _():
                fresh.wait()

            @pl.when((tick > 0) & (s > 0))
            def _():
                block(h).wait_recv()

            @pl.loop(0, half)
            def _(i):
                f = h * half + i
                values = jnp.where(f < live, raw[tick, f].astype(f32), 0.0)
                put(x1, 2 + f, 0, normed(values, first_gain[...]))

            @pl.when((tick == 0) & (h == 0))
            def _():
                for copy in loads[0]:
                    copy.wait()
                for copy in loads[2] + loads[3]:
                    copy.start()

            acc[h, :, 1 : cols + 1] = part(x1, w1, h, [(a, 0, 1) for a in range(3)], 0)

        def first_end(h):
            @pl.when((tick == 0) & (h == 0))
            def _():
                for side in range(2):
                    @pl.when(takes_from[side])
                    def _(side=side):
                        for copy in start_edges(side):
                            copy.wait_recv()

                for window, rows in ((x1, fcache_edge), (x2, scache_edge)):
                    for f in range(2):
                        put_shifted(window, f, rows[0, f], rows[1, f], lambda pair: pair)

                for copy in loads[1]:
                    copy.wait()

            @pl.when((tick > 0) & (s == 0) & (h == 0))
            def _():
                for side in range(2):
                    @pl.when(takes_from[side])
                    def _(side=side):
                        fresh_edge(side).wait_recv()

            @pl.when((tick > 0) & (s > 0))
            def _():
                for side in range(2):
                    @pl.when(takes_from[side])
                    def _(side=side):
                        block_edge(h, side).wait_recv()

            @pl.loop(0, half)
            def _(i):
                f = h * half + i
                put_shifted(
                    x1, 2 + f, raw_edge[tick, 0, f], raw_edge[tick, 1, f],
                    lambda pair: normed(jnp.where(f < live, pair, 0.0), first_gain[...]),
                )

            acc[h, :, 1 : cols + 1] += part(
                x1, w1, h, [(a, 1, 3) for a in range(3)], len(first_a)
            )

            @pl.loop(0, half)
            def _(i):
                f = h * half + i
                hidden = jnp.where(f < live, summed(h, i, first_bias[...]), 0.0)
                values = normed(hidden, second_gain[...])
                second_in[tick, f] = values.astype(bf16)
                put(x2, 2 + f, 0, values)

            for side in range(2):
                @pl.when(sends_to[side])
                def _(side=side):
                    second_rows(tick, h, side).start()

        @pl.loop(0, 4)
        def _(slot):
            ending = jnp.where(tick == 0, slot // 2, slot % 2)
            h = jnp.where(tick == 0, slot % 2, slot // 2)

            @pl.when(ending == 0)
            def _():
                first_start(h)

            @pl.when(ending == 1)
            def _():
                first_end(h)

        @pl.loop(0, 2)
        def _(h):
            @pl.when((tick == 0) & (h == 0))
            def _():
                for copy in loads[2]:
                    copy.wait()

            acc[h, :, 1 : cols + 1] = part(x2, w2, h, [(0, 0, 3), (1, 0, 1), (2, 0, 1)], 0)

            for side in range(2):
                @pl.when(takes_from[side])
                def _(side=side):
                    second_rows(tick, h, side).wait_recv()

            @pl.loop(0, half)
            def _(i):
                f = h * half + i
                put_shifted(
                    x2, 2 + f, second_edge[tick, 0, f], second_edge[tick, 1, f], lambda pair: pair
                )

            @pl.when((tick == 0) & (h == 0))
            def _():
                for copy in loads[3]:
                    copy.wait()

            acc[h, :, 1 : cols + 1] += part(x2, w2, h, [(1, 1, 3), (2, 1, 3)], len(second_a))

            @pl.loop(0, half)
            def _(i):
                f = h * half + i
                total = summed(h, i, second_bias[...]) + raw[tick, f].astype(f32)
                out[tick, 0, f] = jnp.where(f < live, total, 0.0).astype(bf16)

            @pl.when((tick == 0) & (s < sections - 1))
            def _():
                block(h).start()
                for side in range(2):
                    @pl.when(sends_to[side])
                    def _(side=side):
                        block_edge(h, side).start()

        for window in (x1, x2):
            for j in range(2):
                window[j] = window[live + j]

    for window, target in ((x1, first_out), (x2, second_out)):
        for j in range(2):
            values = window[j, :, 0:channels].astype(f32)
            target[0, j] = values.reshape(cols, height, channels).astype(bf16)

    for side in range(2):
        @pl.when(sends_to[side])
        def _(side=side):
            for copy in start_edges(side):
                copy.wait_send()

            @pl.loop(0, ticks)
            def _(tick):
                for h in range(2):
                    second_rows(tick, h, side).wait_send()

            @pl.when(s == 0)
            def _():
                fresh_edge(side).wait_send()

            @pl.when(s < sections - 1)
            def _():
                for h in range(2):
                    block_edge(h, side).wait_send()

    @pl.when(s < sections - 1)
    def _():
        for h in range(2):
            block(h).wait_send()


def deliver(*refs):
    sem = refs[-1]
    copies = [
        pltpu.make_async_copy(refs[k], refs[3 + k], sem.at[k]) for k in range(3)
    ]
    for copy in copies:
        copy.start()
    for copy in copies:
        copy.wait()


def swapped(array):
    return jnp.swapaxes(array, -3, -2)


def on_device(
    held_blocks, incoming, frame_counts, first_cache, second_cache, first_kernel, first_bias,
    first_gain, second_kernel, second_bias, second_gain,
):
    held_blocks, incoming, first_cache, second_cache = (
        swapped(v) for v in (held_blocks, incoming, first_cache, second_cache)
    )
    _, frames, cols, height, channels = held_blocks.shape
    ticks = incoming.shape[0] + 1
    bf16 = jnp.bfloat16
    anywhere = pl.BlockSpec(memory_space=pltpu.HBM)
    inside = pl.BlockSpec(memory_space=pltpu.VMEM)
    shapes = (
        jax.ShapeDtypeStruct((ticks, 1, frames, cols, height, channels), bf16),
        jax.ShapeDtypeStruct(first_cache.shape, bf16),
        jax.ShapeDtypeStruct(second_cache.shape, bf16),
    )
    transfers = 14 + 4 * ticks
    results = pl.pallas_call(
        kernel,
        out_shape=tuple(pltpu.VMEM(v.shape, v.dtype) for v in shapes),
        in_specs=[pl.BlockSpec(memory_space=pltpu.SMEM)] + [anywhere] * 5
        + [inside, inside, anywhere, inside, inside],
        out_specs=(inside, inside, inside),
        scratch_shapes=[
            pltpu.VMEM((ticks, frames, cols, height, channels), bf16),
            pltpu.VMEM((ticks, 2, frames, cols, 2, channels), bf16),
            pltpu.VMEM((2, cols, height, channels), bf16),
            pltpu.VMEM((2, 2, cols, 2, channels), bf16),
            pltpu.VMEM((2, cols, height, channels), bf16),
            pltpu.VMEM((2, 2, cols, 2, channels), bf16),
            pltpu.VMEM((ticks, frames, cols, height, channels), bf16),
            pltpu.VMEM((ticks, 2, frames, cols, 2, channels), bf16),
            pltpu.VMEM((frames + 2, cols * height, 3 * channels), bf16),
            pltpu.VMEM((frames + 2, cols * height, 3 * channels), bf16),
            pltpu.VMEM((9 * channels, 3 * channels), bf16),
            pltpu.VMEM((9 * channels, 3 * channels), bf16),
            pltpu.VMEM((2, frames // 2, cols + 2, height, 3 * channels), jnp.float32),
            pltpu.SemaphoreType.DMA((4,)),
            pltpu.SemaphoreType.DMA((4,)),
            pltpu.SemaphoreType.DMA((transfers,)),
            pltpu.SemaphoreType.DMA((transfers,)),
        ],
        compiler_params=pltpu.CompilerParams(
            collective_id=0, has_side_effects=True, vmem_limit_bytes=60 * 1024 * 1024
        ),
    )(
        frame_counts, held_blocks, incoming, first_cache, second_cache, first_kernel, first_bias,
        first_gain, second_kernel, second_bias, second_gain,
    )
    results = pl.pallas_call(
        deliver,
        out_shape=shapes,
        in_specs=[inside] * 3,
        out_specs=(anywhere,) * 3,
        scratch_shapes=[pltpu.SemaphoreType.DMA((3,))],
        compiler_params=pltpu.CompilerParams(vmem_limit_bytes=4 * 1024 * 1024),
    )(*results)
    return tuple(swapped(v) for v in results)


def solution(mesh):
    return jax.shard_map(
        on_device,
        mesh=mesh,
        in_specs=(
            P("segment", None, "strip", None, None),
            P(None, None, "strip", None, None),
            P(),
            P("segment", None, "strip", None, None),
            P("segment", None, "strip", None, None),
            P("segment", None, None, None, None, None),
            P("segment", None),
            P("segment", None),
            P("segment", None, None, None, None, None),
            P("segment", None),
            P("segment", None),
        ),
        out_specs=(
            P(None, "segment", None, "strip", None, None),
            P("segment", None, "strip", None, None),
            P("segment", None, "strip", None, None),
        ),
        check_vma=False,
    )
```

```python
import jax
import jax.numpy as jnp
from jax import lax
from jax.experimental import pallas as pl
from jax.experimental.pallas import tpu as pltpu
from jax.sharding import PartitionSpec as P

EPSILON = 1e-06
MESH = pl.DeviceIdType.MESH


def normed(values, channel_gain):
    factor = lax.rsqrt(jnp.mean(values * values, axis=-1, keepdims=True) + EPSILON)
    half = values * factor * (0.5 * channel_gain)
    return half + half * jnp.tanh(half)


def with_neighbours(values, above, below):
    height = values.shape[1]
    row = lax.broadcasted_iota(jnp.int32, values.shape[:2] + (1,), 1)
    down = jnp.where(row == 0, above, pltpu.roll(values, 1, 1))
    up = jnp.where(row == height - 1, below, pltpu.roll(values, height - 1, 1))
    return down, up


def kernel(
    counts, held, incoming, first_cache, second_cache, first_kernel, first_bias, first_gain,
    second_kernel, second_bias, second_gain, out, first_out, second_out,
    raw, raw_edge, fcache, fcache_edge, scache, scache_edge, second_edge, packed, second_packed,
    x1, x2, w1, w2, acc, local_sem, w_sem, send_sem, recv_sem,
):
    ticks, frames, cols, height, channels = (out.shape[i] for i in (0, 2, 3, 4, 5))
    half = frames // 2
    sections, strips = lax.axis_size("segment"), lax.axis_size("strip")
    s, p = lax.axis_index("segment"), lax.axis_index("strip")
    has_above, has_below = p > 0, p < strips - 1
    f32, bf16 = jnp.float32, jnp.bfloat16

    local = [
        pltpu.make_async_copy(held.at[0], raw.at[0], local_sem.at[0]),
        pltpu.make_async_copy(first_cache.at[0], fcache, local_sem.at[1]),
        pltpu.make_async_copy(second_cache.at[0], scache, local_sem.at[2]),
    ]
    for copy in local:
        copy.start()
    fresh = pltpu.make_async_copy(incoming.at[0], raw.at[1], local_sem.at[3])

    def weights(source, target, which, blocks, start):
        return [
            pltpu.make_async_copy(
                source.at[0, a, b, c],
                target.at[pl.ds((start + k) * channels, channels), pl.ds(c * channels, channels)],
                w_sem.at[which],
            )
            for k, (a, b) in enumerate(blocks)
            for c in range(3)
        ]

    first_a = [(0, 1), (1, 1), (2, 1)]
    first_b = [(a, b) for a in range(3) for b in (0, 2)]
    second_a = [(0, 1), (0, 0), (0, 2), (1, 1), (2, 1)]
    second_b = [(a, b) for a in (1, 2) for b in (0, 2)]
    loads = [
        weights(first_kernel, w1, 0, first_a, 0),
        weights(first_kernel, w1, 1, first_b, len(first_a)),
        weights(second_kernel, w2, 2, second_a, 0),
        weights(second_kernel, w2, 3, second_b, len(second_a)),
    ]
    around = [(i, j) for i in (-1, 0, 1) for j in (-1, 0, 1) if (i, j) != (0, 0)]
    barrier = pltpu.get_barrier_semaphore()

    def exists(i, j):
        return (s + i >= 0) & (s + i < sections) & (p + j >= 0) & (p + j < strips)

    for i, j in around:
        @pl.when(exists(i, j))
        def _(i=i, j=j):
            pl.semaphore_signal(barrier, inc=1, device_id=(s + i, p + j), device_id_type=MESH)

    for copy in loads[0]:
        copy.start()

    def remote(source, target, k, i, j):
        return pltpu.make_async_remote_copy(
            src_ref=source, dst_ref=target, send_sem=send_sem.at[k], recv_sem=recv_sem.at[k],
            device_id=(s + i, p + j), device_id_type=MESH,
        )

    def edge(source, target, side, k, i):
        rows = pl.ds(side * half, half)
        return remote(source.at[side], target.at[:, rows], k + side, i, 1 - 2 * side)

    edge_targets = [
        fcache_edge, raw_edge.at[0, 0], raw_edge.at[0, 1], scache_edge, raw_edge.at[1, 0],
        raw_edge.at[1, 1],
    ]

    def start_edge(kind, side):
        return edge(packed.at[kind], edge_targets[kind], side, 2 * kind, 0)

    def pack(target, frames_of):
        height_row = lax.broadcasted_iota(jnp.int32, (cols, height, 1), 1)
        for side in range(2):
            rows = None
            for k, values in enumerate(frames_of):
                shift = (k + 1 - side) % height
                moved = pltpu.roll(values, shift, 1) if shift else values
                rows = moved if rows is None else jnp.where(height_row == k, moved, rows)
            target[side] = rows[:, 0:half].astype(bf16)

    def span(h):
        return pl.ds(h * half, half)

    def block(h):
        return remote(out.at[0, 0, span(h)], raw.at[1, span(h)], 12 + h, 1, 0)

    def block_edge(h, side):
        return edge(packed.at[6 + h], raw_edge.at[1, h], side, 14 + 2 * h, 1)

    def second_rows(tick, h, side):
        k = 18 + 4 * tick + 2 * h
        return edge(second_packed.at[tick, h], second_edge.at[tick, h], side, k, 0)

    sends_to = (has_below, has_above)
    takes_from = (has_above, has_below)

    def each_side(existing, act):
        for side in range(2):
            @pl.when(existing[side])
            def _(side=side):
                act(side)

    def pack_start(kind):
        source = {0: fcache, 1: raw.at[0, span(0)], 2: raw.at[0, span(1)], 3: scache}[kind]
        pack(packed.at[kind], [source[k].astype(f32) for k in range(half)])

    for side in range(2):
        @pl.when(jnp.logical_not(takes_from[side]))
        def _(side=side):
            rows = slice(side * half, (side + 1) * half)
            zeros = jnp.zeros((cols, half, channels), bf16)
            fcache_edge[:, rows] = zeros
            scache_edge[:, rows] = zeros
            for tick in range(ticks):
                for h in range(2):
                    raw_edge[tick, h, :, rows] = zeros
                    second_edge[tick, h, :, rows] = zeros

    for copy in local:
        copy.wait()
    pack_start(0)
    pack_start(1)
    pl.semaphore_wait(barrier, sum(exists(i, j).astype(jnp.int32) for i, j in around))
    for kind in range(2):
        each_side(sends_to, lambda side: start_edge(kind, side).start())
    pack_start(2)
    pack_start(3)
    for kind in range(2, 4):
        each_side(sends_to, lambda side: start_edge(kind, side).start())

    @pl.when(s == 0)
    def _():
        fresh.start()

    for copy in loads[1]:
        copy.start()

    for h in range(2):
        for at in (0, cols + 1):
            acc[h, :, at] = jnp.zeros((half, height, 3 * channels), f32)

    def put(window, f, plane, values):
        flat = values.reshape(cols * height, channels).astype(bf16)
        window[f, :, plane * channels : (plane + 1) * channels] = flat

    def put_shifted(window, first, edges, prepare):
        rows = prepare(edges.astype(f32))
        for k in range(half):
            values = window[first + k, :, 0:channels].astype(f32).reshape(cols, height, channels)
            down, up = with_neighbours(
                values, rows[:, k : k + 1], rows[:, half + k : half + k + 1]
            )
            put(window, first + k, 1, down)
            put(window, first + k, 2, up)

    for window, cache in ((x1, fcache), (x2, scache)):
        for f in range(2):
            put(window, f, 0, cache[f].astype(f32))

    def part(window, matrix, h, pieces, start):
        lhs = jnp.concatenate(
            [
                window[pl.ds(h * half + a, half), :, first * channels : last * channels].reshape(
                    half * cols * height, (last - first) * channels
                )
                for a, first, last in pieces
            ],
            axis=-1,
        )
        rows = matrix[start * channels : start * channels + lhs.shape[-1]]
        product = jnp.dot(lhs, rows, preferred_element_type=f32)
        return product.reshape(half, cols, height, 3 * channels)

    def summed(h, f, bias):
        return (
            acc[h, f, 0:cols, :, 0:channels]
            + acc[h, f, 1 : cols + 1, :, channels : 2 * channels]
            + acc[h, f, 2 : cols + 2, :, 2 * channels : 3 * channels]
            + bias
        )

    @pl.loop(0, ticks)
    def _(tick):
        live = counts[sections - 1 - s + tick]

        def first_start(h):
            @pl.when((tick > 0) & (s > 0))
            def _():
                block(h).wait_recv()

            @pl.loop(0, half)
            def _(i):
                f = h * half + i
                values = jnp.where(f < live, raw[tick, f].astype(f32), 0.0)
                put(x1, 2 + f, 0, normed(values, first_gain[...]))

            @pl.when((tick == 0) & (h == 0))
            def _():
                for copy in loads[0]:
                    copy.wait()
                for copy in loads[2] + loads[3]:
                    copy.start()

            acc[h, :, 1 : cols + 1] = part(x1, w1, h, [(a, 0, 1) for a in range(3)], 0)

        def first_end(h):
            @pl.when((tick == 0) & (h == 0))
            def _():
                for kind in range(2):
                    each_side(takes_from, lambda side: start_edge(kind, side).wait_recv())
                put_shifted(x1, 0, fcache_edge[...], lambda rows: rows)

            @pl.when((tick == 0) & (h == 1))
            def _():
                each_side(takes_from, lambda side: start_edge(2, side).wait_recv())

            for k in range(2):
                @pl.when((tick > 0) & (s == 0) & (h == k))
                def _(k=k):
                    each_side(takes_from, lambda side: start_edge(4 + k, side).wait_recv())

            @pl.when((tick > 0) & (s > 0))
            def _():
                each_side(takes_from, lambda side: block_edge(h, side).wait_recv())

            row = lax.broadcasted_iota(jnp.int32, (cols, 2 * half, 1), 1)
            alive = h * half + row % half < live
            put_shifted(
                x1, 2 + h * half, raw_edge[tick, h],
                lambda rows: normed(jnp.where(alive, rows, 0.0), first_gain[...]),
            )

            @pl.when((tick == 0) & (h == 0))
            def _():
                for copy in loads[1]:
                    copy.wait()

            acc[h, :, 1 : cols + 1] += part(
                x1, w1, h, [(a, 1, 3) for a in range(3)], len(first_a)
            )

            @pl.loop(0, half)
            def _(i):
                f = h * half + i
                hidden = jnp.where(f < live, summed(h, i, first_bias[...]), 0.0)
                put(x2, 2 + f, 0, normed(hidden, second_gain[...]))

            pack(
                second_packed.at[tick, h],
                [
                    x2[2 + h * half + k, :, 0:channels].astype(f32).reshape(cols, height, channels)
                    for k in range(half)
                ],
            )
            each_side(sends_to, lambda side: second_rows(tick, h, side).start())

        @pl.loop(0, 4)
        def _(slot):
            ending = jnp.where(tick == 0, slot // 2, slot % 2)
            h = jnp.where(tick == 0, slot % 2, slot // 2)

            @pl.when(ending == 0)
            def _():
                first_start(h)

            @pl.when(ending == 1)
            def _():
                first_end(h)

        @pl.loop(0, 2)
        def _(h):
            @pl.when((tick == 0) & (h == 0))
            def _():
                for copy in loads[2]:
                    copy.wait()
                each_side(takes_from, lambda side: start_edge(3, side).wait_recv())
                put_shifted(x2, 0, scache_edge[...], lambda rows: rows)

            @pl.when((tick == 0) & (h == 0) & (s == 0))
            def _():
                fresh.wait()
                for k in range(2):
                    pack(
                        packed.at[4 + k],
                        [raw[1, k * half + m].astype(f32) for m in range(half)],
                    )
                    each_side(sends_to, lambda side: start_edge(4 + k, side).start())

            acc[h, :, 1 : cols + 1] = part(x2, w2, h, [(0, 0, 3), (1, 0, 1), (2, 0, 1)], 0)

            each_side(takes_from, lambda side: second_rows(tick, h, side).wait_recv())
            put_shifted(x2, 2 + h * half, second_edge[tick, h], lambda rows: rows)

            @pl.when((tick == 0) & (h == 0))
            def _():
                for copy in loads[3]:
                    copy.wait()

            acc[h, :, 1 : cols + 1] += part(x2, w2, h, [(1, 1, 3), (2, 1, 3)], len(second_a))

            @pl.loop(0, half)
            def _(i):
                f = h * half + i
                total = summed(h, i, second_bias[...]) + raw[tick, f].astype(f32)
                out[tick, 0, f] = jnp.where(f < live, total, 0.0).astype(bf16)

            @pl.when((tick == 0) & (s < sections - 1))
            def _():
                block(h).start()
                pack(
                    packed.at[6 + h],
                    [out[0, 0, h * half + k].astype(f32) for k in range(half)],
                )
                each_side(sends_to, lambda side: block_edge(h, side).start())

        for window in (x1, x2):
            for j in range(2):
                window[j] = window[live + j]

    for window, target in ((x1, first_out), (x2, second_out)):
        for j in range(2):
            values = window[j, :, 0:channels].astype(f32)
            target[0, j] = values.reshape(cols, height, channels).astype(bf16)

    def sent(side):
        for kind in range(4):
            start_edge(kind, side).wait_send()

        @pl.loop(0, ticks)
        def _(tick):
            for h in range(2):
                second_rows(tick, h, side).wait_send()

        @pl.when(s == 0)
        def _():
            for kind in range(4, 6):
                start_edge(kind, side).wait_send()

        @pl.when(s < sections - 1)
        def _():
            for h in range(2):
                block_edge(h, side).wait_send()

    each_side(sends_to, sent)

    @pl.when(s < sections - 1)
    def _():
        for h in range(2):
            block(h).wait_send()


def deliver(*refs):
    sem = refs[-1]
    copies = [
        pltpu.make_async_copy(refs[k], refs[3 + k], sem.at[k]) for k in range(3)
    ]
    for copy in copies:
        copy.start()
    for copy in copies:
        copy.wait()


def swapped(array):
    return jnp.swapaxes(array, -3, -2)


def on_device(
    held_blocks, incoming, frame_counts, first_cache, second_cache, first_kernel, first_bias,
    first_gain, second_kernel, second_bias, second_gain,
):
    held_blocks, incoming, first_cache, second_cache = (
        swapped(v) for v in (held_blocks, incoming, first_cache, second_cache)
    )
    _, frames, cols, height, channels = held_blocks.shape
    ticks = incoming.shape[0] + 1
    bf16 = jnp.bfloat16
    anywhere = pl.BlockSpec(memory_space=pltpu.HBM)
    inside = pl.BlockSpec(memory_space=pltpu.VMEM)
    shapes = (
        jax.ShapeDtypeStruct((ticks, 1, frames, cols, height, channels), bf16),
        jax.ShapeDtypeStruct(first_cache.shape, bf16),
        jax.ShapeDtypeStruct(second_cache.shape, bf16),
    )
    transfers = 18 + 4 * ticks
    results = pl.pallas_call(
        kernel,
        out_shape=tuple(pltpu.VMEM(v.shape, v.dtype) for v in shapes),
        in_specs=[pl.BlockSpec(memory_space=pltpu.SMEM)] + [anywhere] * 5
        + [inside, inside, anywhere, inside, inside],
        out_specs=(inside, inside, inside),
        scratch_shapes=[
            pltpu.VMEM((ticks, frames, cols, height, channels), bf16),
            pltpu.VMEM((ticks, 2, cols, frames, channels), bf16),
            pltpu.VMEM((2, cols, height, channels), bf16),
            pltpu.VMEM((cols, 4, channels), bf16),
            pltpu.VMEM((2, cols, height, channels), bf16),
            pltpu.VMEM((cols, 4, channels), bf16),
            pltpu.VMEM((ticks, 2, cols, frames, channels), bf16),
            pltpu.VMEM((8, 2, cols, frames // 2, channels), bf16),
            pltpu.VMEM((ticks, 2, 2, cols, frames // 2, channels), bf16),
            pltpu.VMEM((frames + 2, cols * height, 3 * channels), bf16),
            pltpu.VMEM((frames + 2, cols * height, 3 * channels), bf16),
            pltpu.VMEM((9 * channels, 3 * channels), bf16),
            pltpu.VMEM((9 * channels, 3 * channels), bf16),
            pltpu.VMEM((2, frames // 2, cols + 2, height, 3 * channels), jnp.float32),
            pltpu.SemaphoreType.DMA((4,)),
            pltpu.SemaphoreType.DMA((4,)),
            pltpu.SemaphoreType.DMA((transfers,)),
            pltpu.SemaphoreType.DMA((transfers,)),
        ],
        compiler_params=pltpu.CompilerParams(
            collective_id=0, has_side_effects=True, vmem_limit_bytes=60 * 1024 * 1024
        ),
    )(
        frame_counts, held_blocks, incoming, first_cache, second_cache, first_kernel, first_bias,
        first_gain, second_kernel, second_bias, second_gain,
    )
    results = pl.pallas_call(
        deliver,
        out_shape=shapes,
        in_specs=[inside] * 3,
        out_specs=(anywhere,) * 3,
        scratch_shapes=[pltpu.SemaphoreType.DMA((3,))],
        compiler_params=pltpu.CompilerParams(vmem_limit_bytes=4 * 1024 * 1024),
    )(*results)
    return tuple(swapped(v) for v in results)


def solution(mesh):
    return jax.shard_map(
        on_device,
        mesh=mesh,
        in_specs=(
            P("segment", None, "strip", None, None),
            P(None, None, "strip", None, None),
            P(),
            P("segment", None, "strip", None, None),
            P("segment", None, "strip", None, None),
            P("segment", None, None, None, None, None),
            P("segment", None),
            P("segment", None),
            P("segment", None, None, None, None, None),
            P("segment", None),
            P("segment", None),
        ),
        out_specs=(
            P(None, "segment", None, "strip", None, None),
            P("segment", None, "strip", None, None),
            P("segment", None, "strip", None, None),
        ),
        check_vma=False,
    )
```

```python
import jax
import jax.numpy as jnp
from jax import lax
from jax.experimental import pallas as pl
from jax.experimental.pallas import tpu as pltpu
from jax.sharding import PartitionSpec as P

EPSILON = 1e-06
MESH = pl.DeviceIdType.MESH


def normed(values, channel_gain):
    factor = lax.rsqrt(jnp.mean(values * values, axis=-1, keepdims=True) + EPSILON)
    half = values * factor * (0.5 * channel_gain)
    return half + half * jnp.tanh(half)


def with_neighbours(values, above, below):
    height = values.shape[1]
    row = lax.broadcasted_iota(jnp.int32, values.shape[:2] + (1,), 1)
    down = jnp.where(row == 0, above, pltpu.roll(values, 1, 1))
    up = jnp.where(row == height - 1, below, pltpu.roll(values, height - 1, 1))
    return down, up


def kernel(
    counts, held, incoming, first_cache, second_cache, first_kernel, first_bias, first_gain,
    second_kernel, second_bias, second_gain, out, first_out, second_out,
    raw, raw_edge, fcache, fcache_edge, scache, scache_edge, second_edge, packed, second_packed,
    x1, x2, w1, w2, acc, local_sem, w_sem, send_sem, recv_sem,
):
    ticks, frames, cols, height, channels = (out.shape[i] for i in (0, 2, 3, 4, 5))
    half = frames // 2
    sections, strips = lax.axis_size("segment"), lax.axis_size("strip")
    s, p = lax.axis_index("segment"), lax.axis_index("strip")
    has_above, has_below = p > 0, p < strips - 1
    f32, bf16 = jnp.float32, jnp.bfloat16

    local = [
        pltpu.make_async_copy(held.at[0], raw.at[0], local_sem.at[0]),
        pltpu.make_async_copy(first_cache.at[0], fcache, local_sem.at[1]),
        pltpu.make_async_copy(second_cache.at[0], scache, local_sem.at[2]),
    ]
    for copy in local:
        copy.start()
    fresh = pltpu.make_async_copy(incoming.at[0], raw.at[1], local_sem.at[3])

    def weights(source, target, which, blocks, start):
        return [
            pltpu.make_async_copy(
                source.at[0, a, b, c],
                target.at[pl.ds((start + k) * channels, channels), pl.ds(c * channels, channels)],
                w_sem.at[which],
            )
            for k, (a, b) in enumerate(blocks)
            for c in range(3)
        ]

    first_a = [(0, 1), (1, 1), (2, 1)]
    first_b = [(a, b) for a in range(3) for b in (0, 2)]
    second_a = [(0, 1), (0, 0), (0, 2), (1, 1), (2, 1)]
    second_b = [(a, b) for a in (1, 2) for b in (0, 2)]
    loads = [
        weights(first_kernel, w1, 0, first_a, 0),
        weights(first_kernel, w1, 1, first_b, len(first_a)),
        weights(second_kernel, w2, 2, second_a, 0),
        weights(second_kernel, w2, 3, second_b, len(second_a)),
    ]
    around = [(i, j) for i in (-1, 0, 1) for j in (-1, 0, 1) if (i, j) != (0, 0)]
    barrier = pltpu.get_barrier_semaphore()

    def exists(i, j):
        return (s + i >= 0) & (s + i < sections) & (p + j >= 0) & (p + j < strips)

    for i, j in around:
        @pl.when(exists(i, j))
        def _(i=i, j=j):
            pl.semaphore_signal(barrier, inc=1, device_id=(s + i, p + j), device_id_type=MESH)

    for copy in loads[0] + loads[1]:
        copy.start()

    def remote(source, target, k, i, j):
        return pltpu.make_async_remote_copy(
            src_ref=source, dst_ref=target, send_sem=send_sem.at[k], recv_sem=recv_sem.at[k],
            device_id=(s + i, p + j), device_id_type=MESH,
        )

    def edge(source, target, side, k, i):
        rows = pl.ds(side * half, half)
        return remote(source.at[side], target.at[:, rows], k + side, i, 1 - 2 * side)

    edge_targets = [
        fcache_edge, raw_edge.at[0, 0], raw_edge.at[0, 1], scache_edge, raw_edge.at[1, 0],
        raw_edge.at[1, 1],
    ]

    def start_edge(kind, side):
        return edge(packed.at[kind], edge_targets[kind], side, 2 * kind, 0)

    def pack(target, frames_of):
        height_row = lax.broadcasted_iota(jnp.int32, (cols, height, 1), 1)
        for side in range(2):
            rows = None
            for k, values in enumerate(frames_of):
                shift = (k + 1 - side) % height
                moved = pltpu.roll(values, shift, 1) if shift else values
                rows = moved if rows is None else jnp.where(height_row == k, moved, rows)
            target[side] = rows[:, 0:half].astype(bf16)

    def span(h):
        return pl.ds(h * half, half)

    def block(h):
        return remote(out.at[0, 0, span(h)], raw.at[1, span(h)], 12 + h, 1, 0)

    def block_edge(h, side):
        return edge(packed.at[6 + h], raw_edge.at[1, h], side, 14 + 2 * h, 1)

    def second_rows(tick, h, side):
        k = 18 + 4 * tick + 2 * h
        return edge(second_packed.at[tick, h], second_edge.at[tick, h], side, k, 0)

    sends_to = (has_below, has_above)
    takes_from = (has_above, has_below)

    def each_side(existing, act):
        for side in range(2):
            @pl.when(existing[side])
            def _(side=side):
                act(side)

    def pack_start(kind):
        source = {0: fcache, 1: raw.at[0, span(0)], 2: raw.at[0, span(1)], 3: scache}[kind]
        pack(packed.at[kind], [source[k].astype(f32) for k in range(half)])

    for side in range(2):
        @pl.when(jnp.logical_not(takes_from[side]))
        def _(side=side):
            rows = slice(side * half, (side + 1) * half)
            zeros = jnp.zeros((cols, half, channels), bf16)
            fcache_edge[:, rows] = zeros
            scache_edge[:, rows] = zeros
            for tick in range(ticks):
                for h in range(2):
                    raw_edge[tick, h, :, rows] = zeros
                    second_edge[tick, h, :, rows] = zeros

    for copy in local:
        copy.wait()
    pack_start(0)
    pack_start(1)
    pl.semaphore_wait(barrier, sum(exists(i, j).astype(jnp.int32) for i, j in around))
    for kind in range(2):
        each_side(sends_to, lambda side: start_edge(kind, side).start())
    pack_start(2)
    pack_start(3)
    for kind in range(2, 4):
        each_side(sends_to, lambda side: start_edge(kind, side).start())

    @pl.when(s == 0)
    def _():
        fresh.start()

    for h in range(2):
        for at in (0, cols + 1):
            acc[h, :, at] = jnp.zeros((half, height, 3 * channels), f32)

    def put(window, f, plane, values):
        flat = values.reshape(cols * height, channels).astype(bf16)
        window[f, :, plane * channels : (plane + 1) * channels] = flat

    def put_shifted(window, first, edges, prepare):
        rows = prepare(edges.astype(f32))
        for k in range(half):
            values = window[first + k, :, 0:channels].astype(f32).reshape(cols, height, channels)
            down, up = with_neighbours(
                values, rows[:, k : k + 1], rows[:, half + k : half + k + 1]
            )
            put(window, first + k, 1, down)
            put(window, first + k, 2, up)

    for window, cache in ((x1, fcache), (x2, scache)):
        for f in range(2):
            put(window, f, 0, cache[f].astype(f32))

    def part(window, matrix, h, pieces, start):
        lhs = jnp.concatenate(
            [
                window[pl.ds(h * half + a, half), :, first * channels : last * channels].reshape(
                    half * cols * height, (last - first) * channels
                )
                for a, first, last in pieces
            ],
            axis=-1,
        )
        rows = matrix[start * channels : start * channels + lhs.shape[-1]]
        product = jnp.dot(lhs, rows, preferred_element_type=f32)
        return product.reshape(half, cols, height, 3 * channels)

    def summed(h, f, bias):
        return (
            acc[h, f, 0:cols, :, 0:channels]
            + acc[h, f, 1 : cols + 1, :, channels : 2 * channels]
            + acc[h, f, 2 : cols + 2, :, 2 * channels : 3 * channels]
            + bias
        )

    @pl.loop(0, ticks)
    def _(tick):
        live = counts[sections - 1 - s + tick]

        def first_start(h):
            @pl.when((tick == 0) & (h == 0))
            def _():
                for copy in loads[0]:
                    copy.wait()
                for copy in loads[2] + loads[3]:
                    copy.start()

            @pl.when((tick > 0) & (s > 0))
            def _():
                block(h).wait_recv()

            for i in range(half):
                f = h * half + i
                values = jnp.where(f < live, raw[tick, f].astype(f32), 0.0)
                put(x1, 2 + f, 0, normed(values, first_gain[...]))

            acc[h, :, 1 : cols + 1] = part(x1, w1, h, [(a, 0, 1) for a in range(3)], 0)

        def first_end(h):
            @pl.when((tick == 0) & (h == 0))
            def _():
                for kind in range(2):
                    each_side(takes_from, lambda side: start_edge(kind, side).wait_recv())
                put_shifted(x1, 0, fcache_edge[...], lambda rows: rows)
                for copy in loads[1]:
                    copy.wait()

            @pl.when((tick == 0) & (h == 1))
            def _():
                each_side(takes_from, lambda side: start_edge(2, side).wait_recv())

            for k in range(2):
                @pl.when((tick > 0) & (s == 0) & (h == k))
                def _(k=k):
                    each_side(takes_from, lambda side: start_edge(4 + k, side).wait_recv())

            @pl.when((tick > 0) & (s > 0))
            def _():
                each_side(takes_from, lambda side: block_edge(h, side).wait_recv())

            row = lax.broadcasted_iota(jnp.int32, (cols, 2 * half, 1), 1)
            alive = h * half + row % half < live
            put_shifted(
                x1, 2 + h * half, raw_edge[tick, h],
                lambda rows: normed(jnp.where(alive, rows, 0.0), first_gain[...]),
            )

            acc[h, :, 1 : cols + 1] += part(
                x1, w1, h, [(a, 1, 3) for a in range(3)], len(first_a)
            )

            for i in range(half):
                f = h * half + i
                hidden = jnp.where(f < live, summed(h, i, first_bias[...]), 0.0)
                put(x2, 2 + f, 0, normed(hidden, second_gain[...]))

            pack(
                second_packed.at[tick, h],
                [
                    x2[2 + h * half + k, :, 0:channels].astype(f32).reshape(cols, height, channels)
                    for k in range(half)
                ],
            )
            each_side(sends_to, lambda side: second_rows(tick, h, side).start())

        @pl.loop(0, 4)
        def _(slot):
            ending = jnp.where(tick == 0, slot // 2, slot % 2)
            h = jnp.where(tick == 0, slot % 2, slot // 2)

            @pl.when(ending == 0)
            def _():
                first_start(h)

            @pl.when(ending == 1)
            def _():
                first_end(h)

        @pl.loop(0, 2)
        def _(h):
            @pl.when((tick == 0) & (h == 0))
            def _():
                for copy in loads[2] + loads[3]:
                    copy.wait()
                each_side(takes_from, lambda side: start_edge(3, side).wait_recv())
                put_shifted(x2, 0, scache_edge[...], lambda rows: rows)

            @pl.when((tick == 0) & (h == 0) & (s == 0))
            def _():
                fresh.wait()
                for k in range(2):
                    pack(
                        packed.at[4 + k],
                        [raw[1, k * half + m].astype(f32) for m in range(half)],
                    )
                    each_side(sends_to, lambda side: start_edge(4 + k, side).start())

            acc[h, :, 1 : cols + 1] = part(x2, w2, h, [(0, 0, 3), (1, 0, 1), (2, 0, 1)], 0)

            each_side(takes_from, lambda side: second_rows(tick, h, side).wait_recv())
            put_shifted(x2, 2 + h * half, second_edge[tick, h], lambda rows: rows)

            acc[h, :, 1 : cols + 1] += part(x2, w2, h, [(1, 1, 3), (2, 1, 3)], len(second_a))

            for i in range(half):
                f = h * half + i
                total = summed(h, i, second_bias[...]) + raw[tick, f].astype(f32)
                out[tick, 0, f] = jnp.where(f < live, total, 0.0).astype(bf16)

            @pl.when((tick == 0) & (s < sections - 1))
            def _():
                block(h).start()
                pack(
                    packed.at[6 + h],
                    [out[0, 0, h * half + k].astype(f32) for k in range(half)],
                )
                each_side(sends_to, lambda side: block_edge(h, side).start())

        for window in (x1, x2):
            for j in range(2):
                window[j] = window[live + j]

    for window, target in ((x1, first_out), (x2, second_out)):
        for j in range(2):
            values = window[j, :, 0:channels].astype(f32)
            target[0, j] = values.reshape(cols, height, channels).astype(bf16)

    def sent(side):
        for kind in range(4):
            start_edge(kind, side).wait_send()

        @pl.loop(0, ticks)
        def _(tick):
            for h in range(2):
                second_rows(tick, h, side).wait_send()

        @pl.when(s == 0)
        def _():
            for kind in range(4, 6):
                start_edge(kind, side).wait_send()

        @pl.when(s < sections - 1)
        def _():
            for h in range(2):
                block_edge(h, side).wait_send()

    each_side(sends_to, sent)

    @pl.when(s < sections - 1)
    def _():
        for h in range(2):
            block(h).wait_send()


def deliver(*refs):
    sem = refs[-1]
    copies = [
        pltpu.make_async_copy(refs[k], refs[3 + k], sem.at[k]) for k in range(3)
    ]
    for copy in copies:
        copy.start()
    for copy in copies:
        copy.wait()


def swapped(array):
    return jnp.swapaxes(array, -3, -2)


def on_device(
    held_blocks, incoming, frame_counts, first_cache, second_cache, first_kernel, first_bias,
    first_gain, second_kernel, second_bias, second_gain,
):
    held_blocks, incoming, first_cache, second_cache = (
        swapped(v) for v in (held_blocks, incoming, first_cache, second_cache)
    )
    _, frames, cols, height, channels = held_blocks.shape
    ticks = incoming.shape[0] + 1
    bf16 = jnp.bfloat16
    anywhere = pl.BlockSpec(memory_space=pltpu.HBM)
    inside = pl.BlockSpec(memory_space=pltpu.VMEM)
    shapes = (
        jax.ShapeDtypeStruct((ticks, 1, frames, cols, height, channels), bf16),
        jax.ShapeDtypeStruct(first_cache.shape, bf16),
        jax.ShapeDtypeStruct(second_cache.shape, bf16),
    )
    transfers = 18 + 4 * ticks
    results = pl.pallas_call(
        kernel,
        out_shape=tuple(pltpu.VMEM(v.shape, v.dtype) for v in shapes),
        in_specs=[pl.BlockSpec(memory_space=pltpu.SMEM)] + [anywhere] * 5
        + [inside, inside, anywhere, inside, inside],
        out_specs=(inside, inside, inside),
        scratch_shapes=[
            pltpu.VMEM((ticks, frames, cols, height, channels), bf16),
            pltpu.VMEM((ticks, 2, cols, frames, channels), bf16),
            pltpu.VMEM((2, cols, height, channels), bf16),
            pltpu.VMEM((cols, 4, channels), bf16),
            pltpu.VMEM((2, cols, height, channels), bf16),
            pltpu.VMEM((cols, 4, channels), bf16),
            pltpu.VMEM((ticks, 2, cols, frames, channels), bf16),
            pltpu.VMEM((8, 2, cols, frames // 2, channels), bf16),
            pltpu.VMEM((ticks, 2, 2, cols, frames // 2, channels), bf16),
            pltpu.VMEM((frames + 2, cols * height, 3 * channels), bf16),
            pltpu.VMEM((frames + 2, cols * height, 3 * channels), bf16),
            pltpu.VMEM((9 * channels, 3 * channels), bf16),
            pltpu.VMEM((9 * channels, 3 * channels), bf16),
            pltpu.VMEM((2, frames // 2, cols + 2, height, 3 * channels), jnp.float32),
            pltpu.SemaphoreType.DMA((4,)),
            pltpu.SemaphoreType.DMA((4,)),
            pltpu.SemaphoreType.DMA((transfers,)),
            pltpu.SemaphoreType.DMA((transfers,)),
        ],
        compiler_params=pltpu.CompilerParams(
            collective_id=0, has_side_effects=True, vmem_limit_bytes=60 * 1024 * 1024
        ),
    )(
        frame_counts, held_blocks, incoming, first_cache, second_cache, first_kernel, first_bias,
        first_gain, second_kernel, second_bias, second_gain,
    )
    results = pl.pallas_call(
        deliver,
        out_shape=shapes,
        in_specs=[inside] * 3,
        out_specs=(anywhere,) * 3,
        scratch_shapes=[pltpu.SemaphoreType.DMA((3,))],
        compiler_params=pltpu.CompilerParams(vmem_limit_bytes=4 * 1024 * 1024),
    )(*results)
    return tuple(swapped(v) for v in results)


def solution(mesh):
    return jax.shard_map(
        on_device,
        mesh=mesh,
        in_specs=(
            P("segment", None, "strip", None, None),
            P(None, None, "strip", None, None),
            P(),
            P("segment", None, "strip", None, None),
            P("segment", None, "strip", None, None),
            P("segment", None, None, None, None, None),
            P("segment", None),
            P("segment", None),
            P("segment", None, None, None, None, None),
            P("segment", None),
            P("segment", None),
        ),
        out_specs=(
            P(None, "segment", None, "strip", None, None),
            P("segment", None, "strip", None, None),
            P("segment", None, "strip", None, None),
        ),
        check_vma=False,
    )
```

```python
import jax
import jax.numpy as jnp
from jax import lax
from jax.experimental import pallas as pl
from jax.experimental.pallas import tpu as pltpu
from jax.sharding import PartitionSpec as P

EPSILON = 1e-06
MESH = pl.DeviceIdType.MESH


def normed(values, channel_gain):
    factor = lax.rsqrt(jnp.mean(values * values, axis=-1, keepdims=True) + EPSILON)
    half = values * factor * (0.5 * channel_gain)
    return half + half * jnp.tanh(half)


def with_neighbours(values, above, below):
    height = values.shape[1]
    row = lax.broadcasted_iota(jnp.int32, values.shape[:2] + (1,), 1)
    down = jnp.where(row == 0, above, pltpu.roll(values, 1, 1))
    up = jnp.where(row == height - 1, below, pltpu.roll(values, height - 1, 1))
    return down, up


def kernel(
    counts_in, held, incoming, first_cache, second_cache, first_kernel, first_bias_in,
    first_gain_in, second_kernel, second_bias_in, second_gain_in, out, first_out, second_out,
    counts, first_bias, first_gain, second_bias, second_gain,
    raw, raw_edge, fcache, fcache_edge, scache, scache_edge, second_edge, packed, second_packed,
    x1, x2, w1, w2, acc, local_sem, w_sem, send_sem, recv_sem,
):
    ticks, frames, cols, height, channels = (out.shape[i] for i in (0, 2, 3, 4, 5))
    half = frames // 2
    sections, strips = lax.axis_size("segment"), lax.axis_size("strip")
    s, p = lax.axis_index("segment"), lax.axis_index("strip")
    has_above, has_below = p > 0, p < strips - 1
    f32, bf16 = jnp.float32, jnp.bfloat16

    local = [
        pltpu.make_async_copy(held.at[0], raw.at[0], local_sem.at[0]),
        pltpu.make_async_copy(first_cache.at[0], fcache, local_sem.at[1]),
        pltpu.make_async_copy(second_cache.at[0], scache, local_sem.at[2]),
    ]
    small = [
        (counts_in, counts), (first_bias_in, first_bias), (first_gain_in, first_gain),
        (second_bias_in, second_bias), (second_gain_in, second_gain),
    ]
    local += [
        pltpu.make_async_copy(source, target, local_sem.at[4 + k])
        for k, (source, target) in enumerate(small)
    ]
    for copy in local:
        copy.start()
    fresh = pltpu.make_async_copy(incoming.at[0], raw.at[1], local_sem.at[3])

    def weights(source, target, which, blocks, start):
        return [
            pltpu.make_async_copy(
                source.at[0, a, b, c],
                target.at[pl.ds((start + k) * channels, channels), pl.ds(c * channels, channels)],
                w_sem.at[which],
            )
            for k, (a, b) in enumerate(blocks)
            for c in range(3)
        ]

    first_a = [(0, 1), (1, 1), (2, 1)]
    first_b = [(a, b) for a in range(3) for b in (0, 2)]
    second_a = [(0, 1), (0, 0), (0, 2), (1, 1), (2, 1)]
    second_b = [(a, b) for a in (1, 2) for b in (0, 2)]
    loads = [
        weights(first_kernel, w1, 0, first_a, 0),
        weights(first_kernel, w1, 1, first_b, len(first_a)),
        weights(second_kernel, w2, 2, second_a, 0),
        weights(second_kernel, w2, 3, second_b, len(second_a)),
    ]
    around = [(i, j) for i in (-1, 0, 1) for j in (-1, 0, 1) if (i, j) != (0, 0)]
    barrier = pltpu.get_barrier_semaphore()

    def exists(i, j):
        return (s + i >= 0) & (s + i < sections) & (p + j >= 0) & (p + j < strips)

    for i, j in around:
        @pl.when(exists(i, j))
        def _(i=i, j=j):
            pl.semaphore_signal(barrier, inc=1, device_id=(s + i, p + j), device_id_type=MESH)

    for copy in loads[0] + loads[1]:
        copy.start()

    def remote(source, target, k, i, j):
        return pltpu.make_async_remote_copy(
            src_ref=source, dst_ref=target, send_sem=send_sem.at[k], recv_sem=recv_sem.at[k],
            device_id=(s + i, p + j), device_id_type=MESH,
        )

    def edge(source, target, side, k, i):
        rows = pl.ds(side * half, half)
        return remote(source.at[side], target.at[:, rows], k + side, i, 1 - 2 * side)

    edge_targets = [
        fcache_edge, raw_edge.at[0, 0], raw_edge.at[0, 1], scache_edge, raw_edge.at[1, 0],
        raw_edge.at[1, 1],
    ]

    def start_edge(kind, side):
        return edge(packed.at[kind], edge_targets[kind], side, 2 * kind, 0)

    def pack(target, frames_of):
        height_row = lax.broadcasted_iota(jnp.int32, (cols, height, 1), 1)
        for side in range(2):
            rows = None
            for k, values in enumerate(frames_of):
                shift = (k + 1 - side) % height
                moved = pltpu.roll(values, shift, 1) if shift else values
                rows = moved if rows is None else jnp.where(height_row == k, moved, rows)
            target[side] = rows[:, 0:half].astype(bf16)

    def span(h):
        return pl.ds(h * half, half)

    def block(h):
        return remote(out.at[0, 0, span(h)], raw.at[1, span(h)], 12 + h, 1, 0)

    def block_edge(h, side):
        return edge(packed.at[6 + h], raw_edge.at[1, h], side, 14 + 2 * h, 1)

    def second_rows(tick, h, side):
        k = 18 + 4 * tick + 2 * h
        return edge(second_packed.at[tick, h], second_edge.at[tick, h], side, k, 0)

    sends_to = (has_below, has_above)
    takes_from = (has_above, has_below)

    def each_side(existing, act):
        for side in range(2):
            @pl.when(existing[side])
            def _(side=side):
                act(side)

    def pack_start(kind):
        source = {0: fcache, 1: raw.at[0, span(0)], 2: raw.at[0, span(1)], 3: scache}[kind]
        pack(packed.at[kind], [source[k].astype(f32) for k in range(half)])

    for side in range(2):
        @pl.when(jnp.logical_not(takes_from[side]))
        def _(side=side):
            rows = slice(side * half, (side + 1) * half)
            zeros = jnp.zeros((cols, half, channels), bf16)
            fcache_edge[:, rows] = zeros
            scache_edge[:, rows] = zeros
            for tick in range(ticks):
                for h in range(2):
                    raw_edge[tick, h, :, rows] = zeros
                    second_edge[tick, h, :, rows] = zeros

    for copy in local:
        copy.wait()
    pack_start(0)
    pack_start(1)
    pl.semaphore_wait(barrier, sum(exists(i, j).astype(jnp.int32) for i, j in around))
    for kind in range(2):
        each_side(sends_to, lambda side: start_edge(kind, side).start())
    pack_start(2)
    pack_start(3)
    for kind in range(2, 4):
        each_side(sends_to, lambda side: start_edge(kind, side).start())

    @pl.when(s == 0)
    def _():
        fresh.start()

    for h in range(2):
        for at in (0, cols + 1):
            acc[h, :, at] = jnp.zeros((half, height, 3 * channels), f32)

    def put(window, f, plane, values):
        flat = values.reshape(cols * height, channels).astype(bf16)
        window[f, :, plane * channels : (plane + 1) * channels] = flat

    def put_shifted(window, first, edges, prepare):
        rows = prepare(edges.astype(f32))
        for k in range(half):
            values = window[first + k, :, 0:channels].astype(f32).reshape(cols, height, channels)
            down, up = with_neighbours(
                values, rows[:, k : k + 1], rows[:, half + k : half + k + 1]
            )
            put(window, first + k, 1, down)
            put(window, first + k, 2, up)

    for window, cache in ((x1, fcache), (x2, scache)):
        for f in range(2):
            put(window, f, 0, cache[f].astype(f32))

    def part(window, matrix, h, pieces, start):
        lhs = jnp.concatenate(
            [
                window[pl.ds(h * half + a, half), :, first * channels : last * channels].reshape(
                    half * cols * height, (last - first) * channels
                )
                for a, first, last in pieces
            ],
            axis=-1,
        )
        rows = matrix[start * channels : start * channels + lhs.shape[-1]]
        product = jnp.dot(lhs, rows, preferred_element_type=f32)
        return product.reshape(half, cols, height, 3 * channels)

    def summed(h, f, bias):
        return (
            acc[h, f, 0:cols, :, 0:channels]
            + acc[h, f, 1 : cols + 1, :, channels : 2 * channels]
            + acc[h, f, 2 : cols + 2, :, 2 * channels : 3 * channels]
            + bias
        )

    @pl.loop(0, ticks)
    def _(tick):
        live = counts[sections - 1 - s + tick]

        def first_start(h):
            @pl.when((tick == 0) & (h == 0))
            def _():
                for copy in loads[0]:
                    copy.wait()
                for copy in loads[2] + loads[3]:
                    copy.start()

            @pl.when((tick > 0) & (s > 0))
            def _():
                block(h).wait_recv()

            for i in range(half):
                f = h * half + i
                values = jnp.where(f < live, raw[tick, f].astype(f32), 0.0)
                put(x1, 2 + f, 0, normed(values, first_gain[...]))

            acc[h, :, 1 : cols + 1] = part(x1, w1, h, [(a, 0, 1) for a in range(3)], 0)

        def first_end(h):
            @pl.when((tick == 0) & (h == 0))
            def _():
                for kind in range(2):
                    each_side(takes_from, lambda side: start_edge(kind, side).wait_recv())
                put_shifted(x1, 0, fcache_edge[...], lambda rows: rows)
                for copy in loads[1]:
                    copy.wait()

            @pl.when((tick == 0) & (h == 1))
            def _():
                each_side(takes_from, lambda side: start_edge(2, side).wait_recv())

            for k in range(2):
                @pl.when((tick > 0) & (s == 0) & (h == k))
                def _(k=k):
                    each_side(takes_from, lambda side: start_edge(4 + k, side).wait_recv())

            @pl.when((tick > 0) & (s > 0))
            def _():
                each_side(takes_from, lambda side: block_edge(h, side).wait_recv())

            row = lax.broadcasted_iota(jnp.int32, (cols, 2 * half, 1), 1)
            alive = h * half + row % half < live
            put_shifted(
                x1, 2 + h * half, raw_edge[tick, h],
                lambda rows: normed(jnp.where(alive, rows, 0.0), first_gain[...]),
            )

            acc[h, :, 1 : cols + 1] += part(
                x1, w1, h, [(a, 1, 3) for a in range(3)], len(first_a)
            )

            for i in range(half):
                f = h * half + i
                hidden = jnp.where(f < live, summed(h, i, first_bias[...]), 0.0)
                put(x2, 2 + f, 0, normed(hidden, second_gain[...]))

            pack(
                second_packed.at[tick, h],
                [
                    x2[2 + h * half + k, :, 0:channels].astype(f32).reshape(cols, height, channels)
                    for k in range(half)
                ],
            )
            each_side(sends_to, lambda side: second_rows(tick, h, side).start())

        @pl.loop(0, 4)
        def _(slot):
            ending = jnp.where(tick == 0, slot // 2, slot % 2)
            h = jnp.where(tick == 0, slot % 2, slot // 2)

            @pl.when(ending == 0)
            def _():
                first_start(h)

            @pl.when(ending == 1)
            def _():
                first_end(h)

        @pl.loop(0, 2)
        def _(h):
            @pl.when((tick == 0) & (h == 0))
            def _():
                for copy in loads[2] + loads[3]:
                    copy.wait()
                each_side(takes_from, lambda side: start_edge(3, side).wait_recv())
                put_shifted(x2, 0, scache_edge[...], lambda rows: rows)

            @pl.when((tick == 0) & (h == 0) & (s == 0))
            def _():
                fresh.wait()
                for k in range(2):
                    pack(
                        packed.at[4 + k],
                        [raw[1, k * half + m].astype(f32) for m in range(half)],
                    )
                    each_side(sends_to, lambda side: start_edge(4 + k, side).start())

            acc[h, :, 1 : cols + 1] = part(x2, w2, h, [(0, 0, 3), (1, 0, 1), (2, 0, 1)], 0)

            each_side(takes_from, lambda side: second_rows(tick, h, side).wait_recv())
            put_shifted(x2, 2 + h * half, second_edge[tick, h], lambda rows: rows)

            acc[h, :, 1 : cols + 1] += part(x2, w2, h, [(1, 1, 3), (2, 1, 3)], len(second_a))

            for i in range(half):
                f = h * half + i
                total = summed(h, i, second_bias[...]) + raw[tick, f].astype(f32)
                out[tick, 0, f] = jnp.where(f < live, total, 0.0).astype(bf16)

            @pl.when((tick == 0) & (s < sections - 1))
            def _():
                block(h).start()
                pack(
                    packed.at[6 + h],
                    [out[0, 0, h * half + k].astype(f32) for k in range(half)],
                )
                each_side(sends_to, lambda side: block_edge(h, side).start())

        for window in (x1, x2):
            for j in range(2):
                window[j] = window[live + j]

    for window, target in ((x1, first_out), (x2, second_out)):
        for j in range(2):
            values = window[j, :, 0:channels].astype(f32)
            target[0, j] = values.reshape(cols, height, channels).astype(bf16)

    def sent(side):
        for kind in range(4):
            start_edge(kind, side).wait_send()

        @pl.loop(0, ticks)
        def _(tick):
            for h in range(2):
                second_rows(tick, h, side).wait_send()

        @pl.when(s == 0)
        def _():
            for kind in range(4, 6):
                start_edge(kind, side).wait_send()

        @pl.when(s < sections - 1)
        def _():
            for h in range(2):
                block_edge(h, side).wait_send()

    each_side(sends_to, sent)

    @pl.when(s < sections - 1)
    def _():
        for h in range(2):
            block(h).wait_send()


def deliver(*refs):
    sem = refs[-1]
    copies = [
        pltpu.make_async_copy(refs[k], refs[3 + k], sem.at[k]) for k in range(3)
    ]
    for copy in copies:
        copy.start()
    for copy in copies:
        copy.wait()


def swapped(array):
    return jnp.swapaxes(array, -3, -2)


def on_device(
    held_blocks, incoming, frame_counts, first_cache, second_cache, first_kernel, first_bias,
    first_gain, second_kernel, second_bias, second_gain,
):
    held_blocks, incoming, first_cache, second_cache = (
        swapped(v) for v in (held_blocks, incoming, first_cache, second_cache)
    )
    _, frames, cols, height, channels = held_blocks.shape
    ticks = incoming.shape[0] + 1
    bf16 = jnp.bfloat16
    anywhere = pl.BlockSpec(memory_space=pltpu.HBM)
    inside = pl.BlockSpec(memory_space=pltpu.VMEM)
    shapes = (
        jax.ShapeDtypeStruct((ticks, 1, frames, cols, height, channels), bf16),
        jax.ShapeDtypeStruct(first_cache.shape, bf16),
        jax.ShapeDtypeStruct(second_cache.shape, bf16),
    )
    transfers = 18 + 4 * ticks
    results = pl.pallas_call(
        kernel,
        out_shape=tuple(pltpu.VMEM(v.shape, v.dtype) for v in shapes),
        in_specs=[anywhere] * 11,
        out_specs=(inside, inside, inside),
        scratch_shapes=[
            pltpu.SMEM(frame_counts.shape, frame_counts.dtype),
            *(pltpu.VMEM((1, channels), jnp.float32) for _ in range(4)),
            pltpu.VMEM((ticks, frames, cols, height, channels), bf16),
            pltpu.VMEM((ticks, 2, cols, frames, channels), bf16),
            pltpu.VMEM((2, cols, height, channels), bf16),
            pltpu.VMEM((cols, 4, channels), bf16),
            pltpu.VMEM((2, cols, height, channels), bf16),
            pltpu.VMEM((cols, 4, channels), bf16),
            pltpu.VMEM((ticks, 2, cols, frames, channels), bf16),
            pltpu.VMEM((8, 2, cols, frames // 2, channels), bf16),
            pltpu.VMEM((ticks, 2, 2, cols, frames // 2, channels), bf16),
            pltpu.VMEM((frames + 2, cols * height, 3 * channels), bf16),
            pltpu.VMEM((frames + 2, cols * height, 3 * channels), bf16),
            pltpu.VMEM((9 * channels, 3 * channels), bf16),
            pltpu.VMEM((9 * channels, 3 * channels), bf16),
            pltpu.VMEM((2, frames // 2, cols + 2, height, 3 * channels), jnp.float32),
            pltpu.SemaphoreType.DMA((9,)),
            pltpu.SemaphoreType.DMA((4,)),
            pltpu.SemaphoreType.DMA((transfers,)),
            pltpu.SemaphoreType.DMA((transfers,)),
        ],
        compiler_params=pltpu.CompilerParams(
            collective_id=0, has_side_effects=True, vmem_limit_bytes=60 * 1024 * 1024
        ),
    )(
        frame_counts, held_blocks, incoming, first_cache, second_cache, first_kernel, first_bias,
        first_gain, second_kernel, second_bias, second_gain,
    )
    results = pl.pallas_call(
        deliver,
        out_shape=shapes,
        in_specs=[inside] * 3,
        out_specs=(anywhere,) * 3,
        scratch_shapes=[pltpu.SemaphoreType.DMA((3,))],
        compiler_params=pltpu.CompilerParams(vmem_limit_bytes=4 * 1024 * 1024),
    )(*results)
    return tuple(swapped(v) for v in results)


def solution(mesh):
    return jax.shard_map(
        on_device,
        mesh=mesh,
        in_specs=(
            P("segment", None, "strip", None, None),
            P(None, None, "strip", None, None),
            P(),
            P("segment", None, "strip", None, None),
            P("segment", None, "strip", None, None),
            P("segment", None, None, None, None, None),
            P("segment", None),
            P("segment", None),
            P("segment", None, None, None, None, None),
            P("segment", None),
            P("segment", None),
        ),
        out_specs=(
            P(None, "segment", None, "strip", None, None),
            P("segment", None, "strip", None, None),
            P("segment", None, "strip", None, None),
        ),
        check_vma=False,
    )
```
